256 devices in a mesh: row: 16 (over y_lo, x, core), col: 16 (over y_hi, z).
Axes of the slice: x: 4, y: 4 (y_hi: 2, y_lo: 2; y = y_hi * 2 + y_lo), z: 8, core: 2. Of those that a mesh axis runs over, the one named last changes fastest.
Arguments:
- amplitudes: bfloat16 [32, 32, 256, 256], P('row', 'col'), may hold values from -6 to 6
- coulomb: bfloat16 [32, 32, 256, 256], P('row', 'col'), may hold values from -12 to 12
- fit_ov: bfloat16 [1024, 32, 256], P(None, 'col'), may hold values from -0.25 to 0.25
- fit_vv: bfloat16 [16, 256, 256], P('row'), may hold values from -0.5 to 0.5
- eps_occ: float32 [32], replicated, may hold values from -2 to -0.5
- eps_vir: float32 [256], replicated, may hold values from 0.5 to 2.5
Outputs:
- updated: bfloat16 [32, 32, 256, 256], P('row', 'col')
The draws below stay inside these ranges and needn't reach their ends.
All inputs are finite; a program needn't handle non-finite values.
Results may differ from the reference program's by a relative error of at most 0.009.
Values may be sent and summed in bfloat16 or wider, within the bound.
A program may use at most 64 MiB of HBM per device.

```python
import jax
import jax.numpy as jnp
from jax import lax

O = 32
V = 256
X = 1024
QL = 16
ITERS = 2


def levels(own_key, dims, split, least, high):
    def one(position, blocks):
        steps = jax.random.uniform(jax.random.fold_in(jax.random.fold_in(own_key, 6), position), (blocks,), jnp.float32, least / len(split), high / len(split))
        return jnp.repeat(jnp.exp(steps), dims[position] // blocks).reshape((-1,) + (1,) * (len(dims) - position - 1))

    gain = one(*split[0])
    for cut in split[1:]:
        gain = gain * one(*cut)
    return gain


def centred(own_key, shape, scale, limit, cuts=(), held_as=jnp.bfloat16):
    level = levels(own_key, shape, cuts, -0.22, 0.18) if cuts else 1.0
    array = jax.random.normal(own_key, shape, jnp.float32) * scale * level
    return jnp.minimum(jnp.maximum(array, -limit), limit).astype(held_as)


def setup_inputs(seed: int = 0) -> dict:
    key_list = jax.random.split(jax.random.key(seed), 7)
    amplitudes = centred(key_list[0], (O, O, V, V), 1.0, 6.0, ((0, 16), (1, 16)))
    coulomb = centred(key_list[1], (O, O, V, V), 2.0, 12.0, ((0, 16), (1, 16)))
    fit_ov = centred(key_list[2], (X, O, V), ((X * O * V) ** -0.25), 0.25, ((1, 16),))
    fit_vv = centred(key_list[3], (QL, V, V), ((QL * V * V) ** -0.25), 0.5, ((0, 16),))
    eps_occ = jnp.clip(jax.random.uniform(key_list[4], (O,), jnp.float32, -2.0, -0.5), -2.0, -0.5)
    eps_vir = jnp.clip(jax.random.uniform(key_list[5], (V,), jnp.float32, 0.5, 2.5), 0.5, 2.5)
    return dict(amplitudes=amplitudes, coulomb=coulomb, fit_ov=fit_ov, fit_vv=fit_vv, eps_occ=eps_occ, eps_vir=eps_vir)


def reference(amplitudes, coulomb, fit_ov, fit_vv, eps_occ, eps_vir):
    denominator = (eps_occ[:, None, None, None] + eps_occ[None, :, None, None]
                   - eps_vir[None, None, :, None] - eps_vir[None, None, None, :])
    current = amplitudes
    fit_wide = fit_ov.astype(jnp.float32)
    for sweep in range(ITERS):
        flattened = current.reshape(O * O, V, V).astype(jnp.float32)

        def add_auxiliary(running, fitting):
            fitting = fitting.astype(jnp.float32)
            contracted = jnp.einsum("ac,pcd->pad", fitting, flattened).astype(jnp.bfloat16)
            running = running + jnp.einsum("pad,bd->pab", contracted.astype(jnp.float32), fitting)
            return running, None

        initial = jnp.zeros((O * O, V, V), jnp.float32)
        ladder, unused = lax.scan(add_auxiliary, initial, fit_vv)
        ladder = ladder.reshape(O, O, V, V)
        cycle_partial = jnp.einsum("qkc,ikac->qia", fit_wide, current.astype(jnp.float32)).astype(jnp.bfloat16)
        cycle_term = jnp.einsum("qia,qjb->ijab", cycle_partial.astype(jnp.float32), fit_wide).astype(jnp.bfloat16)
        swapped = jnp.transpose(cycle_term, (1, 0, 3, 2))
        summed = coulomb.astype(jnp.float32) + ladder + cycle_term.astype(jnp.float32) + swapped.astype(jnp.float32)
        current = (summed / denominator).astype(jnp.bfloat16)
    return current
```

```python
import jax
import jax.numpy as jnp
from jax import lax
from jax.sharding import PartitionSpec as P

ITERS = 2


def body(amplitudes, coulomb, fit_ov, fit_vv, eps_occ, eps_vir):
    occ_local, occ_other, virtual, _ = amplitudes.shape
    n = lax.axis_size("row")
    occ_rows = lax.dynamic_slice_in_dim(eps_occ, lax.axis_index("row") * occ_local, occ_local)
    occ_cols = lax.dynamic_slice_in_dim(eps_occ, lax.axis_index("col") * occ_other, occ_other)
    denominator = (
        occ_rows[:, None, None, None]
        + occ_cols[None, :, None, None]
        - eps_vir[None, None, :, None]
        - eps_vir[None, None, None, :]
    )
    fitting = lax.all_gather(fit_vv, "row", axis=0, tiled=True)
    swap = [(r * n + c, c * n + r) for r in range(n) for c in range(n)]
    current = amplitudes
    for sweep in range(ITERS):
        partial_value = jnp.einsum(
            "qkc,ikac->qia", fit_ov, current, preferred_element_type=jnp.float32
        ).astype(jnp.bfloat16)
        piece = lax.psum_scatter(partial_value, "col", scatter_dimension=0, tiled=True)
        cycle_partial = lax.all_gather(piece, "col", axis=0, tiled=True)
        flat = current.reshape(occ_local * occ_other, virtual, virtual)
        contracted = jnp.einsum(
            "qac,pcd->paqd", fitting, flat, preferred_element_type=jnp.float32
        ).astype(jnp.bfloat16)
        ladder = jnp.einsum(
            "paqd,qbd->pab", contracted, fitting, preferred_element_type=jnp.float32
        ).reshape(occ_local, occ_other, virtual, virtual)
        cycle_term = jnp.einsum(
            "qia,qjb->ijab", cycle_partial, fit_ov, preferred_element_type=jnp.float32
        ).astype(jnp.bfloat16)
        moved = lax.ppermute(cycle_term, ("row", "col"), swap)
        returned = jnp.transpose(moved, (1, 0, 3, 2))
        summed = (
            coulomb.astype(jnp.float32)
            + ladder
            + cycle_term.astype(jnp.float32)
            + returned.astype(jnp.float32)
        )
        current = (summed / denominator).astype(jnp.bfloat16)
    return current


def solution(mesh):
    in_specs = (
        P("row", "col", None, None),
        P("row", "col", None, None),
        P(None, "col", None),
        P("row", None, None),
        P(),
        P(),
    )
    out_specs = P("row", "col", None, None)
    return jax.shard_map(body, mesh=mesh, in_specs=in_specs, out_specs=out_specs, check_vma=False)
```

```python
import jax
import jax.numpy as jnp
from jax import lax
from jax.experimental import pallas as pl
from jax.experimental.pallas import tpu as pltpu
from jax.sharding import PartitionSpec as P

ITERS = 2
MESH = pl.DeviceIdType.MESH
F32 = jnp.float32
BF16 = jnp.bfloat16

ZN = 8
XN = 4
RIGHT, LEFT = 0, 1
SUBS = 4
FP = 8


def nn(a, b):
    return jnp.dot(a, b, preferred_element_type=F32)


def nt(a, b):
    return lax.dot_general(a, b, (((1,), (1,)), ((), ())), preferred_element_type=F32)


def tt(a, b):
    return lax.dot_general(a, b, (((0,), (1,)), ((), ())), preferred_element_type=F32)


def kernel(occ, amp, coul, fit, own_b, ev_row, ev_col, out,
           t2, part, rs, yv, yr, pp, fr, bs, acc, con,
           rs_sem, y_sem, ag_sem, bc_sem, f_sem, b_sem,
           rs_send, y_send, ag_send, bc_send, f_send, b_send, local_sem):
    row = lax.axis_index("row")
    col = lax.axis_index("col")
    core = lax.rem(row, 2)
    x = lax.rem(row // 2, XN)
    yl = row // (2 * XN)
    z = lax.rem(col, ZN)
    yh = col // ZN

    def dev(yl_, x_, core_, yh_, z_):
        return (yl_ * (2 * XN) + x_ * 2 + core_, yh_ * ZN + z_)

    z_next = dev(yl, x, core, yh, lax.rem(z + 1, ZN))
    z_prev = dev(yl, x, core, yh, lax.rem(z + ZN - 1, ZN))
    x_next = dev(yl, lax.rem(x + 1, XN), core, yh, z)
    x_prev = dev(yl, lax.rem(x + XN - 1, XN), core, yh, z)
    y_far = dev(yl, x, core, 1 - yh, z)
    y_near = dev(1 - yl, x, core, yh, z)
    y_both = dev(1 - yl, x, core, 1 - yh, z)
    mate = dev(yl, x, 1 - core, yh, z)

    barrier = pltpu.get_barrier_semaphore()
    for peer in (z_next, z_prev, x_next, x_prev, y_far, y_near, y_both, mate):
        pl.semaphore_signal(barrier, inc=1, device_id=peer, device_id_type=MESH)
    pl.semaphore_wait(barrier, 8)

    def send(src, dst, send_sem, recv_sem, peer):
        pltpu.make_async_remote_copy(
            src_ref=src, dst_ref=dst, send_sem=send_sem, recv_sem=recv_sem,
            device_id=peer, device_id_type=MESH,
        ).start()

    def arrived(ref, sem):
        pltpu.make_async_copy(ref, ref, sem).wait()

    chunk = part.shape[1] // ZN
    sub = chunk // SUBS
    half = chunk // 2
    virtual = amp.shape[2]
    f_rows = fit.shape[0] // (2 * FP)
    ring = {RIGHT: z_next, LEFT: z_prev}

    def rows_of(o, s):
        return pl.ds(pl.multiple_of(o * chunk + s * sub, sub), sub)

    z_seed = 2 * x + core
    far_plane = (yl != yh).astype(jnp.int32)
    d_right = lax.rem(z + ZN - z_seed, ZN)
    d_left = lax.rem(z_seed + ZN - z, ZN)
    is_seed = z == z_seed

    def f_ref(ref, way, p):
        return ref.at[pl.ds(pl.multiple_of((way * FP + p) * f_rows, f_rows), f_rows)]

    @pl.when(jnp.logical_and(is_seed, far_plane == 0))
    def _():
        own = pltpu.make_async_copy(fit, fr, local_sem)
        own.start()
        own.wait()

    @pl.when(jnp.logical_and(is_seed, far_plane == 1))
    def _():
        for way in (RIGHT, LEFT):
            for p in range(FP):
                send(f_ref(fit, way, p), f_ref(fr, way, p), f_send.at[2], f_sem.at[way, p], y_both)

    def f_step(k):
        for way, d in ((RIGHT, d_right), (LEFT, d_left)):
            p = k - d - far_plane

            @pl.when(jnp.logical_and(p >= 0, p < FP))
            def _(way=way, d=d, p=p):
                ref = f_ref(fr, way, p)

                @pl.when(jnp.logical_or(d > 0, far_plane == 1))
                def _():
                    arrived(ref, f_sem.at[way, p])

                @pl.when(d < ZN - 1)
                def _():
                    send(ref, ref, f_send.at[way], f_sem.at[way, p], ring[way])

    def pair(x_):
        return bs.at[pl.ds(core * 8 + x_ * 2, 2)]

    def block(x_, yl_):
        return bs.at[pl.ds(core * 8 + x_ * 2 + yl_, 1)]

    x_up = lax.rem(x + 1, XN)
    x_down = lax.rem(x + XN - 1, XN)
    x_two = lax.rem(x + 2, XN)

    def b_step(k):
        @pl.when(k == 0)
        def _():
            send(own_b, block(x, yl), b_send.at[0], b_sem.at[0], y_near)
            own = pltpu.make_async_copy(own_b, block(x, yl), local_sem)
            own.start()
            own.wait()

        @pl.when(k == 1)
        def _():
            arrived(block(x, 1 - yl), b_sem.at[0])
            send(pair(x), pair(x), b_send.at[1], b_sem.at[1], x_next)
            send(pair(x), pair(x), b_send.at[2], b_sem.at[2], x_prev)

        @pl.when(k == 2)
        def _():
            arrived(pair(x_down), b_sem.at[1])
            arrived(pair(x_up), b_sem.at[2])
            send(block(x_down, yl), block(x_down, yl), b_send.at[3], b_sem.at[3], x_next)
            send(block(x_up, 1 - yl), block(x_up, 1 - yl), b_send.at[4], b_sem.at[4], x_prev)

        @pl.when(k == 3)
        def _():
            arrived(block(x_two, yl), b_sem.at[3])
            arrived(block(x_two, 1 - yl), b_sem.at[4])
            lane = bs.at[pl.ds(core * 8, 8)]
            send(lane, lane, b_send.at[5], b_sem.at[5], mate)

    dx = lax.rem(x + XN - z // 2, XN)
    on_lane = core == lax.rem(z, 2)
    on_plane = jnp.logical_and(on_lane, yl == yh)
    is_src = jnp.logical_and(on_plane, dx == 0)
    sel = 1 - is_src.astype(jnp.int32)
    depth = (
        jnp.where(dx == 2, 2, jnp.where(dx == 0, 0, 1))
        + (yl != yh).astype(jnp.int32)
        + jnp.logical_not(on_lane).astype(jnp.int32)
    )

    for i in range(2):
        for j in range(2):
            t2[i * virtual:(i + 1) * virtual, j * virtual:(j + 1) * virtual] = amp[i, j]

    @pl.loop(0, ITERS)
    def _(it):
        first = it == 0

        for m in range(2):
            part[it, m * virtual:(m + 1) * virtual, :] = nt(
                t2[m * virtual:(m + 1) * virtual, :], fit[...]
            ).astype(BF16)
        acc[...] = jnp.zeros_like(acc)

        @pl.loop(0, 4)
        def _(h):
            for s in range(SUBS):
                for way, o, late in (
                    (RIGHT, lax.rem(z + 4 - h, ZN), int(s >= 2)),
                    (LEFT, lax.rem(z + 4 + h, ZN), int(s < 2)),
                ):
                    @pl.when(h >= late)
                    def _(way=way, o=o, late=late, s=s):
                        at = rows_of(o, s)
                        where = pl.ds(s * sub, sub)

                        @pl.when(h > late)
                        def _():
                            slot = rs.at[it, way, h - 1, where]
                            arrived(slot, rs_sem.at[it, way, h - 1, s])
                            part[it, at, :] = (part[it, at, :].astype(F32) + slot[...].astype(F32)).astype(BF16)

                        send(part.at[it, at], rs.at[it, way, h, where], rs_send.at[it],
                             rs_sem.at[it, way, h, s], ring[way])

            @pl.when(first)
            def _():
                f_step(h)
                b_step(h)

        for s in range(SUBS):
            at = rows_of(z, s)
            where = pl.ds(s * sub, sub)
            for way in (RIGHT, LEFT):
                arrived(rs.at[it, way, 3, where], rs_sem.at[it, way, 3, s])
            yv[it, where, :] = (
                part[it, at, :].astype(F32)
                + rs[it, RIGHT, 3, where, :].astype(F32)
                + rs[it, LEFT, 3, where, :].astype(F32)
            ).astype(BF16)
            send(yv.at[it, where], yr.at[it, where], y_send.at[it], y_sem.at[it, s], y_far)
        for s in range(SUBS):
            at = rows_of(z, s)
            where = pl.ds(s * sub, sub)
            arrived(yr.at[it, where], y_sem.at[it, s])
            pp[it, 0, at, :] = (yv[it, where, :].astype(F32) + yr[it, where, :].astype(F32)).astype(BF16)
            for way in (RIGHT, LEFT):
                send(pp.at[it, 0, at], pp.at[it, 0, at], ag_send.at[it], ag_sem.at[it, way, 0, s], ring[way])

        @pl.loop(0, 9)
        def _(n):
            @pl.when(jnp.logical_and(n >= 1, n <= 4))
            def _():
                for s in range(SUBS):
                    for way, o, most in (
                        (RIGHT, lax.rem(z + ZN - n, ZN), 4 if s < 2 else 3),
                        (LEFT, lax.rem(z + n, ZN), 4 if s >= 2 else 3),
                    ):
                        @pl.when(n <= most)
                        def _(way=way, o=o, most=most, s=s):
                            at = rows_of(o, s)
                            ref = pp.at[it, 0, at]
                            arrived(ref, ag_sem.at[it, way, n - 1, s])

                            @pl.when(n < most)
                            def _():
                                send(ref, ref, ag_send.at[it], ag_sem.at[it, way, n, s], ring[way])

            m = n - depth

            @pl.when(jnp.logical_and(m >= 0, m <= 4))
            def _():
                for hf in range(2):
                    for sign in (0, 1):
                        o = lax.rem(z + ZN - m, ZN) if sign == 0 else lax.rem(z + m, ZN)
                        used = True if sign == 0 else jnp.logical_and(m >= 1, m <= 3)

                        @pl.when(used)
                        def _(o=o, hf=hf):
                            at = pl.ds(pl.multiple_of(o * chunk + hf * half, half), half)
                            src = pp.at[it, sel, at]
                            dst = pp.at[it, 1, at]
                            sem = bc_sem.at[it, o * 2 + hf]

                            @pl.when(sel == 1)
                            def _():
                                arrived(dst, sem)

                            @pl.when(jnp.logical_and(on_plane, jnp.logical_or(dx == 0, (dx == 1) if hf == 0 else False)))
                            def _():
                                send(src, dst, bc_send.at[it, 0], sem, x_next)

                            @pl.when(jnp.logical_and(on_plane, jnp.logical_or(dx == 0, (dx == 3) if hf == 1 else False)))
                            def _():
                                send(src, dst, bc_send.at[it, 1], sem, x_prev)

                            @pl.when(on_plane)
                            def _():
                                send(src, dst, bc_send.at[it, 2], sem, y_near)

                            @pl.when(on_lane)
                            def _():
                                send(src, dst, bc_send.at[it, 3], sem, mate)

            @pl.when(first)
            def _():
                f_step(n + 4)

                @pl.when(n == 2)
                def _():
                    other = bs.at[pl.ds((1 - core) * 8, 8)]
                    arrived(other, b_sem.at[5])

            @pl.when(n < 4)
            def _():
                start = lax.rem(core * 8 + n * 4, 16)
                bb = bs[pl.ds(start, 4)].reshape(4 * virtual, virtual)
                for p in range(4):
                    i, j = p // 2, p % 2
                    con[p] = nn(
                        bb, t2[i * virtual:(i + 1) * virtual, j * virtual:(j + 1) * virtual]
                    ).astype(BF16)
                for p in range(4):
                    total = acc[p]
                    for k in range(4):
                        total = total + nt(con[p, k * virtual:(k + 1) * virtual, :], bb[k * virtual:(k + 1) * virtual])
                    acc[p] = total

            @pl.when(jnp.logical_and(n >= 5, n < 7))
            def _():
                i = n - 5
                term = nn(pp[it, 0, pl.ds(pl.multiple_of(i * virtual, virtual), virtual), :], fit[...])
                for j in range(2):
                    acc[2 * i + j] += term[:, j * virtual:(j + 1) * virtual]

        @pl.when(first)
        def _():
            @pl.loop(13, 16)
            def _(k):
                f_step(k)

        for i in range(2):
            term = tt(fr[:, i * virtual:(i + 1) * virtual], pp[it, sel])
            for j in range(2):
                total = coul[i, j].astype(F32) + acc[2 * i + j] + term[:, j * virtual:(j + 1) * virtual]
                denominator = occ[i, j] - ev_col[...] - ev_row[...]
                updated = (total / denominator).astype(BF16)
                t2[i * virtual:(i + 1) * virtual, j * virtual:(j + 1) * virtual] = updated
                out[i, j] = updated

        sent = part.at[it, pl.ds(0, 7 * chunk)]
        arrived(sent, rs_send.at[it])
        arrived(sent, ag_send.at[it])
        arrived(yv.at[it], y_send.at[it])
        whole = pp.at[it, 0]
        fewer = pp.at[it, 0, pl.ds(0, 4 * chunk)]
        for way, near in ((0, 1), (1, 3)):
            @pl.when(is_src)
            def _(way=way):
                arrived(whole, bc_send.at[it, way])

            @pl.when(jnp.logical_and(on_plane, dx == near))
            def _(way=way):
                arrived(fewer, bc_send.at[it, way])

        @pl.when(on_plane)
        def _():
            arrived(whole, bc_send.at[it, 2])

        @pl.when(on_lane)
        def _():
            arrived(whole, bc_send.at[it, 3])

    f_half = fr.at[pl.ds(0, FP * f_rows)]
    for way, d in ((RIGHT, d_right), (LEFT, d_left)):
        @pl.when(d < ZN - 1)
        def _(way=way):
            arrived(f_half, f_send.at[way])

    @pl.when(jnp.logical_and(is_seed, far_plane == 1))
    def _():
        arrived(fr, f_send.at[2])

    arrived(block(x, yl), b_send.at[0])
    arrived(pair(x), b_send.at[1])
    arrived(pair(x), b_send.at[2])
    arrived(block(x, yl), b_send.at[3])
    arrived(block(x, yl), b_send.at[4])
    arrived(bs.at[pl.ds(core * 8, 8)], b_send.at[5])


def body(amplitudes, coulomb, fit_ov, fit_vv, eps_occ, eps_vir):
    occ_local, occ_other, virtual, _ = amplitudes.shape
    aux = fit_ov.shape[0]
    side = occ_local * virtual
    chunk = side // ZN
    occ_rows = lax.dynamic_slice_in_dim(eps_occ, lax.axis_index("row") * occ_local, occ_local)
    occ_cols = lax.dynamic_slice_in_dim(eps_occ, lax.axis_index("col") * occ_other, occ_other)
    occ = occ_rows[:, None] + occ_cols[None, :]
    fit = fit_ov.reshape(aux, occ_other * virtual)
    batch = fit_vv.shape[0] * lax.axis_size("row")
    vmem = pl.BlockSpec(memory_space=pltpu.VMEM)
    dma = pltpu.SemaphoreType.DMA
    return pl.pallas_call(
        kernel,
        out_shape=jax.ShapeDtypeStruct(amplitudes.shape, BF16),
        in_specs=[pl.BlockSpec(memory_space=pltpu.SMEM)] + [vmem] * 6,
        out_specs=vmem,
        scratch_shapes=[
            pltpu.VMEM((side, occ_other * virtual), BF16),
            pltpu.VMEM((ITERS, side, aux), BF16),
            pltpu.VMEM((ITERS, 2, 4, chunk, aux), BF16),
            pltpu.VMEM((ITERS, chunk, aux), BF16),
            pltpu.VMEM((ITERS, chunk, aux), BF16),
            pltpu.VMEM((ITERS, 2, side, aux), BF16),
            pltpu.VMEM((aux, side), BF16),
            pltpu.VMEM((batch, virtual, virtual), BF16),
            pltpu.VMEM((occ_local * occ_other, virtual, virtual), F32),
            pltpu.VMEM((4, 4 * virtual, virtual), BF16),
            dma((ITERS, 2, 4, SUBS)),
            dma((ITERS, SUBS)),
            dma((ITERS, 2, 4, SUBS)),
            dma((ITERS, 2 * ZN)),
            dma((2, FP)),
            dma((6,)),
            dma((ITERS,)),
            dma((ITERS,)),
            dma((ITERS,)),
            dma((ITERS, 4)),
            dma((3,)),
            dma((6,)),
            dma,
        ],
        compiler_params=pltpu.CompilerParams(
            collective_id=0, has_side_effects=True, vmem_limit_bytes=60 * 2**20
        ),
        name="sweeps",
    )(occ, amplitudes, coulomb, fit, fit_vv, eps_vir[None, :], eps_vir[:, None])


def solution(mesh):
    in_specs = (
        P("row", "col", None, None),
        P("row", "col", None, None),
        P(None, "col", None),
        P("row", None, None),
        P(),
        P(),
    )
    out_specs = P("row", "col", None, None)
    return jax.shard_map(body, mesh=mesh, in_specs=in_specs, out_specs=out_specs, check_vma=False)
```

```python
import jax
import jax.numpy as jnp
from jax import lax
from jax.experimental import pallas as pl
from jax.experimental.pallas import tpu as pltpu
from jax.sharding import PartitionSpec as P

ITERS = 2
MESH = pl.DeviceIdType.MESH
F32 = jnp.float32
BF16 = jnp.bfloat16

ZN = 8
XN = 4
RIGHT, LEFT = 0, 1
F_OVER = 9
FP = 4


def nn(a, b):
    return jnp.dot(a, b, preferred_element_type=F32)


def nt(a, b):
    return lax.dot_general(a, b, (((1,), (1,)), ((), ())), preferred_element_type=F32)


def tt(a, b):
    return lax.dot_general(a, b, (((0,), (1,)), ((), ())), preferred_element_type=F32)


def kernel(eps, amp, coul, fit, own_b, ev_row, out,
           t2, part, rsa, rsb, yfirst, yv, yr, pp, fr, bs, acc, con, ev_col,
           rsa_sem, rsb_sem, y_sem, aga_sem, agb_sem, bc_sem, f_sem, b_sem,
           rs_send, y_send, ag_send, bc_send, f_send, b_send, local_sem):
    row = lax.axis_index("row")
    col = lax.axis_index("col")
    core = lax.rem(row, 2)
    x = lax.rem(row // 2, XN)
    yl = row // (2 * XN)
    z = lax.rem(col, ZN)
    yh = col // ZN

    def dev(yl_, x_, core_, yh_, z_):
        return (yl_ * (2 * XN) + x_ * 2 + core_, yh_ * ZN + z_)

    z_next = dev(yl, x, core, yh, lax.rem(z + 1, ZN))
    z_prev = dev(yl, x, core, yh, lax.rem(z + ZN - 1, ZN))
    x_next = dev(yl, lax.rem(x + 1, XN), core, yh, z)
    x_prev = dev(yl, lax.rem(x + XN - 1, XN), core, yh, z)
    y_far = dev(yl, x, core, 1 - yh, z)
    y_near = dev(1 - yl, x, core, yh, z)
    y_both = dev(1 - yl, x, core, 1 - yh, z)
    mate = dev(yl, x, 1 - core, yh, z)

    z_next2 = dev(yl, x, core, yh, lax.rem(z + 2, ZN))
    z_prev2 = dev(yl, x, core, yh, lax.rem(z + ZN - 2, ZN))
    near_mate = dev(1 - yl, x, 1 - core, yh, z)
    far_plane = (yl != yh).astype(jnp.int32)

    def plane_peer(flip, shift):
        yl_ = jnp.where(flip == 1, 1 - yl, yl)
        yh_ = jnp.where(flip == 1, 1 - yh, yh)
        return dev(yl_, lax.rem(x + shift, XN), core, yh_, z)

    barrier = pltpu.get_barrier_semaphore()
    peers = [z_next, z_prev, z_next2, z_prev2, y_far, y_near, near_mate, mate]
    peers += [plane_peer(0, shift) for shift in range(1, XN)] + [plane_peer(1, shift) for shift in range(XN)]
    for peer in peers:
        pl.semaphore_signal(barrier, inc=1, device_id=peer, device_id_type=MESH)
    pl.semaphore_wait(barrier, len(peers))

    def send(src, dst, send_sem, recv_sem, peer):
        pltpu.make_async_remote_copy(
            src_ref=src, dst_ref=dst, send_sem=send_sem, recv_sem=recv_sem,
            device_id=peer, device_id_type=MESH,
        ).start()

    def arrived(ref, sem):
        pltpu.make_async_copy(ref, ref, sem).wait()

    virtual = amp.shape[2]
    side = part.shape[1]
    sub = side // (4 * ZN)
    f_rows = fit.shape[0] // (4 * FP)
    ring = {RIGHT: z_next, LEFT: z_prev}
    ring2 = {RIGHT: z_next2, LEFT: z_prev2}
    toward = {RIGHT: 1, LEFT: ZN - 1}
    even = lax.rem(z, 2) == 0
    b_long = {RIGHT: even, LEFT: jnp.logical_not(even)}

    def a_rows(o, s):
        return pl.ds(pl.multiple_of((o * 2 + s) * sub, sub), sub)

    def b_rows(v, o):
        return pl.ds(pl.multiple_of(side // 2 + v * (side // 4) + o * sub, sub), sub)

    z_seed = 2 * x + core
    d_right = lax.rem(z + ZN - z_seed, ZN)
    d_left = lax.rem(z_seed + ZN - z, ZN)
    is_seed = z == z_seed

    def f_ref(ref, v, way, p):
        return ref.at[pl.ds(pl.multiple_of(((v * 2 + way) * FP + p) * f_rows, f_rows), f_rows)]

    @pl.when(jnp.logical_and(is_seed, far_plane == 0))
    def _():
        ref = pl.ds(pl.multiple_of(yh * 2 * FP * f_rows, f_rows), 2 * FP * f_rows)
        own = pltpu.make_async_copy(fit.at[ref], fr.at[ref], local_sem)
        own.start()
        own.wait()

    def f_seed():
        @pl.when(jnp.logical_and(is_seed, far_plane == 1))
        def _():
            for p in range(FP):
                for way in (RIGHT, LEFT):
                    send(f_ref(fit, 1 - yh, way, p), f_ref(fr, 1 - yh, way, p), f_send.at[2], f_sem.at[0, way, p], y_both)

    def f_delay(d):
        return 2 * d + 2 * far_plane

    def f_over(k):
        for p in range(FP):
            for way, d in ((RIGHT, d_right), (LEFT, d_left)):
                @pl.when(k == jnp.maximum(p + f_delay(d), F_OVER))
                def _(way=way, p=p):
                    ref = f_ref(fr, yh, way, p)
                    send(ref, ref, f_send.at[3], f_sem.at[1, way, p], y_far)

    def f_step(k):
        for way, d in ((RIGHT, d_right), (LEFT, d_left)):
            p = k - f_delay(d)

            @pl.when(jnp.logical_and(p >= 0, p < FP))
            def _(way=way, d=d, p=p):
                ref = f_ref(fr, yh, way, p)

                @pl.when(jnp.logical_or(d > 0, far_plane == 1))
                def _():
                    arrived(ref, f_sem.at[0, way, p])

                @pl.when(d < ZN - 1)
                def _():
                    send(ref, ref, f_send.at[way], f_sem.at[0, way, p], ring[way])

    def pair(x_):
        return bs.at[pl.ds(core * 8 + x_ * 2, 2)]

    def block(x_, yl_):
        return bs.at[pl.ds(core * 8 + x_ * 2 + yl_, 1)]

    x_up = lax.rem(x + 1, XN)
    x_down = lax.rem(x + XN - 1, XN)
    x_two = lax.rem(x + 2, XN)

    def b_step(k):
        @pl.when(k == 0)
        def _():
            send(own_b, block(x, yl), b_send.at[0], b_sem.at[0], y_near)
            own = pltpu.make_async_copy(own_b, block(x, yl), local_sem)
            own.start()
            own.wait()

        @pl.when(k == 2)
        def _():
            arrived(block(x, 1 - yl), b_sem.at[0])
            send(pair(x), pair(x), b_send.at[1], b_sem.at[1], x_next)
            send(pair(x), pair(x), b_send.at[2], b_sem.at[2], x_prev)

        @pl.when(k == 4)
        def _():
            arrived(pair(x_down), b_sem.at[1])
            arrived(pair(x_up), b_sem.at[2])
            send(block(x_down, yl), block(x_down, yl), b_send.at[3], b_sem.at[3], x_next)
            send(block(x_up, 1 - yl), block(x_up, 1 - yl), b_send.at[4], b_sem.at[4], x_prev)

        @pl.when(k == 6)
        def _():
            arrived(block(x_two, yl), b_sem.at[3])
            arrived(block(x_two, 1 - yl), b_sem.at[4])
            lane = bs.at[pl.ds(core * 8, 8)]
            send(lane, lane, b_send.at[5], b_sem.at[5], mate)

        @pl.when(k == 8)
        def _():
            other = bs.at[pl.ds((1 - core) * 8, 8)]
            arrived(other, b_sem.at[5])

    dx = lax.rem(x + XN - z // 2, XN)
    on_lane = core == lax.rem(z, 2)
    is_src = jnp.logical_and(on_lane, dx == 0)
    is_near_src = jnp.logical_and(is_src, far_plane == 0)
    sel = 1 - is_near_src.astype(jnp.int32)

    for i in range(2):
        for j in range(2):
            t2[i * virtual:(i + 1) * virtual, j * virtual:(j + 1) * virtual] = amp[i, j]
    ev_col[...] = jnp.broadcast_to(ev_row[...], (virtual, virtual)).T

    @pl.loop(0, ITERS)
    def _(it):
        first = it == 0

        quarter = side // 4
        theirs = pl.ds(pl.multiple_of(side // 2 + (1 - yh) * quarter, quarter), quarter)
        mine = pl.ds(pl.multiple_of(side // 2 + yh * quarter, quarter), quarter)
        part[it, theirs, :] = nt(t2[theirs, :], fit[...]).astype(BF16)
        for u in (4, 3, 5, 2, 6, 1, 7, 0):
            o = lax.rem(z + u, ZN)
            send(part.at[it, b_rows(1 - yh, o)], yfirst.at[it, o], y_send.at[it], y_sem.at[it, 0, o], y_far)
        @pl.when(first)
        def _():
            f_seed()

        part[it, 0:side // 2, :] = nt(t2[0:side // 2, :], fit[...]).astype(BF16)

        def there(way, steps):
            return lax.rem(z + steps * toward[way], ZN)

        def add_a(at, way, slot, s):
            ref = rsa.at[it, way, slot, s]
            arrived(ref, rsa_sem.at[it, way, slot, s])
            return ref[...].astype(F32)

        def send_a(at, way, slot, s, peer):
            send(part.at[it, at], rsa.at[it, way, slot, s], rs_send.at[it], rsa_sem.at[it, way, slot, s], peer)

        def add_b(way, slot):
            ref = rsb.at[it, way, slot]
            arrived(ref, rsb_sem.at[it, way, slot])
            return ref[...].astype(F32)

        def send_b(at, way, slot, peer):
            send(part.at[it, at], rsb.at[it, way, slot], rs_send.at[it], rsb_sem.at[it, way, slot], peer)

        def both_halves(at, o):
            arrived(yfirst.at[it, o], y_sem.at[it, 0, o])
            return part[it, at, :].astype(F32) + yfirst[it, o].astype(F32)

        for k in range(4):
            for s in range(2):
                for way in (RIGHT, LEFT):
                    long = s == way
                    if k == 0:
                        if long:
                            send_a(a_rows(there(way, 4), s), way, 0, s, ring2[way])
                        send_a(a_rows(there(way, 3), s), way, 1, s, ring[way])
                    elif k < 3:
                        at = a_rows(there(way, 3 - k), s)
                        total = part[it, at, :].astype(F32) + add_a(at, way, k, s)
                        if k == 1 and long:
                            total = total + add_a(at, way, 0, s)
                        part[it, at, :] = total.astype(BF16)
                        send_a(at, way, k + 1, s, ring[way])
            @pl.when(first)
            def _(k=k):
                f_step(2 * k)

            if k == 0:
                part[it, mine, :] = nt(t2[mine, :], fit[...]).astype(BF16)
                acc[...] = jnp.zeros_like(acc)
            for way in (RIGHT, LEFT):
                if k == 1:
                    @pl.when(b_long[way])
                    def _(way=way):
                        o = there(way, 4)
                        at = b_rows(yh, o)
                        part[it, at, :] = both_halves(at, o).astype(BF16)
                        send_b(at, way, 0, ring2[way])

                    o = there(way, 3)
                    at = b_rows(yh, o)
                    part[it, at, :] = both_halves(at, o).astype(BF16)
                    send_b(at, way, 1, ring[way])
                elif k > 1:
                    o = there(way, 4 - k)
                    at = b_rows(yh, o)
                    total = both_halves(at, o) + add_b(way, k - 1)
                    part[it, at, :] = total.astype(BF16)
                    if k == 2:
                        @pl.when(b_long[way])
                        def _(way=way, at=at):
                            part[it, at, :] = (part[it, at, :].astype(F32) + add_b(way, 0)).astype(BF16)
                    send_b(at, way, k, ring[way])

            @pl.when(first)
            def _(k=k):
                f_step(2 * k + 1)
                b_step(k)

        for s in range(2):
            at = a_rows(z, s)
            for way in (RIGHT, LEFT):
                arrived(rsa.at[it, way, 3, s], rsa_sem.at[it, way, 3, s])
            yv[it, s] = (
                part[it, at, :].astype(F32)
                + rsa[it, RIGHT, 3, s].astype(F32)
                + rsa[it, LEFT, 3, s].astype(F32)
            ).astype(BF16)
            send(yv.at[it, s], yr.at[it, s], y_send.at[it], y_sem.at[it, 1, s], y_far)

        @pl.when(first)
        def _():
            f_step(8)

        def own_sends(ref, sems):
            for way in (RIGHT, LEFT):
                send(ref, ref, ag_send.at[it], sems[way], ring[way])

        def to_far(ref, o):
            send(ref, ref, y_send.at[it], y_sem.at[it, 2, o], y_far)

        at = b_rows(yh, z)
        arrived(yfirst.at[it, z], y_sem.at[it, 0, z])
        for way in (RIGHT, LEFT):
            arrived(rsb.at[it, way, 3], rsb_sem.at[it, way, 3])
        pp[it, 0, at, :] = (
            part[it, at, :].astype(F32) + yfirst[it, z].astype(F32)
            + rsb[it, RIGHT, 3].astype(F32) + rsb[it, LEFT, 3].astype(F32)
        ).astype(BF16)
        own_sends(pp.at[it, 0, at], [agb_sem.at[it, way, 0] for way in (RIGHT, LEFT)])
        to_far(pp.at[it, 0, at], z)
        for s in range(2):
            at = a_rows(z, s)
            arrived(yr.at[it, s], y_sem.at[it, 1, s])
            pp[it, 0, at, :] = (yv[it, s].astype(F32) + yr[it, s].astype(F32)).astype(BF16)
            own_sends(pp.at[it, 0, at], [aga_sem.at[it, way, 0, s] for way in (RIGHT, LEFT)])

        def sent_on(ref, way, n, long, sems):
            @pl.when(n < 3)
            def _():
                send(ref, ref, ag_send.at[it], sems(n), ring[way])

            @pl.when(jnp.logical_and(n == 2, long))
            def _():
                send(ref, ref, ag_send.at[it], sems(3), ring2[way])

        @pl.loop(0, 6)
        def _(n):
            @pl.when(jnp.logical_and(n >= 1, n <= 3))
            def _():
                for way in (RIGHT, LEFT):
                    o = lax.rem(z + n * toward[1 - way], ZN)
                    ref = pp.at[it, 0, b_rows(yh, o)]
                    arrived(ref, agb_sem.at[it, way, n - 1])
                    sent_on(ref, way, n, b_long[way], lambda h, way=way: agb_sem.at[it, way, h])
                    to_far(ref, o)
                for s in range(2):
                    for way in (RIGHT, LEFT):
                        o = lax.rem(z + n * toward[1 - way], ZN)
                        ref = pp.at[it, 0, a_rows(o, s)]
                        arrived(ref, aga_sem.at[it, way, n - 1, s])
                        sent_on(ref, way, n, s == way, lambda h, way=way, s=s: aga_sem.at[it, way, h, s])

            @pl.when(n == 3)
            def _():
                o = lax.rem(z + 4, ZN)
                for way in (RIGHT, LEFT):
                    @pl.when(b_long[way])
                    def _(way=way):
                        ref = pp.at[it, 0, b_rows(yh, o)]
                        arrived(ref, agb_sem.at[it, way, 3])
                        to_far(ref, o)
                    arrived(pp.at[it, 0, a_rows(o, way)], aga_sem.at[it, way, 3, way])

            @pl.when(first)
            def _():
                f_step(9 + 2 * n)
                f_over(9 + 2 * n)

            def group(m, act):
                act(lax.rem(z + ZN - m, ZN))

                @pl.when(m >= 1)
                def _():
                    act(lax.rem(z + m, ZN))

                @pl.when(m == 3)
                def _():
                    act(lax.rem(z + 4, ZN))

            @pl.when(jnp.logical_and(is_src, n <= 3))
            def _():
                def act(o):
                    for at, index in (
                        (a_rows(o, far_plane), far_plane * 16 + o),
                        (b_rows(yh, o), far_plane * 16 + 8 + o),
                    ):
                        src, dst, sem = pp.at[it, 0, at], pp.at[it, 1, at], bc_sem.at[it, index]
                        for shift in range(1, XN):
                            send(src, dst, bc_send.at[it, shift], sem, plane_peer(far_plane, shift))

                        @pl.when(far_plane == 1)
                        def _():
                            send(src, dst, bc_send.at[it, 0], sem, plane_peer(1, 0))

                group(n, act)

            m = n - 2 * sel

            @pl.when(jnp.logical_and(on_lane, jnp.logical_and(m >= 0, m <= 3)))
            def _():
                def act(o):
                    for at, index in (
                        (a_rows(o, far_plane), far_plane * 16 + o),
                        (b_rows(yl, o), far_plane * 16 + 8 + o),
                    ):
                        src, dst, sem = pp.at[it, sel, at], pp.at[it, 1, at], bc_sem.at[it, index]

                        @pl.when(sel == 1)
                        def _():
                            arrived(dst, sem)

                        send(src, dst, bc_send.at[it, 4], sem, y_near)
                        send(src, dst, bc_send.at[it, 5], sem, near_mate)
                        send(src, dst, bc_send.at[it, 6], sem, mate)

                group(m, act)

            @pl.when(first)
            def _():
                f_step(10 + 2 * n)
                f_over(10 + 2 * n)
                b_step(n + 4)

            @pl.when(n >= 2)
            def _():
                start = lax.rem(core * 8 + (n - 2) * 4, 16)
                bb = bs[pl.ds(start, 4)].reshape(4 * virtual, virtual)
                for p in range(4):
                    i, j = p // 2, p % 2
                    con[p] = nn(
                        bb, t2[i * virtual:(i + 1) * virtual, j * virtual:(j + 1) * virtual]
                    ).astype(BF16)
                for p in range(4):
                    total = acc[p]
                    for k in range(4):
                        total = total + nt(con[p, k * virtual:(k + 1) * virtual, :], bb[k * virtual:(k + 1) * virtual])
                    acc[p] = total

            @pl.when(n == 5)
            def _():
                for o in range(ZN):
                    arrived(pp.at[it, 0, b_rows(1 - yh, o)], y_sem.at[it, 2, o])

            @pl.when(n >= 4)
            def _():
                i = n - 4
                term = nn(pp[it, 0, pl.ds(pl.multiple_of(i * virtual, virtual), virtual), :], fit[...])
                for j in range(2):
                    acc[2 * i + j] += term[:, j * virtual:(j + 1) * virtual]

        @pl.when(first)
        def _():
            for way in (RIGHT, LEFT):
                for p in range(FP):
                    arrived(f_ref(fr, 1 - yh, way, p), f_sem.at[1, way, p])

        for path in range(2):
            @pl.when(jnp.logical_or(jnp.logical_not(on_lane), far_plane != path))
            def _(path=path):
                for o in range(ZN):
                    arrived(pp.at[it, 1, a_rows(o, path)], bc_sem.at[it, path * 16 + o])
                    half = yh if path == 0 else 1 - yh
                    arrived(pp.at[it, 1, b_rows(half, o)], bc_sem.at[it, path * 16 + 8 + o])

        for i in range(2):
            term = tt(fr[:, i * virtual:(i + 1) * virtual], pp[it, sel])
            for j in range(2):
                total = coul[i, j].astype(F32) + acc[2 * i + j] + term[:, j * virtual:(j + 1) * virtual]
                denominator = (eps[row * 2 + i] + eps[col * 2 + j]) - ev_col[...] - ev_row[...]
                updated = (total / denominator).astype(BF16)
                t2[i * virtual:(i + 1) * virtual, j * virtual:(j + 1) * virtual] = updated
                out[i, j] = updated

        def left(pieces, sem):
            arrived(part.at[it, pl.ds(0, pieces * sub)], sem)

        left(21, rs_send.at[it])
        left(21, ag_send.at[it])
        left(18, y_send.at[it])

        @pl.when(on_lane)
        def _():
            for way in range(4, 7):
                left(16, bc_send.at[it, way])

        @pl.when(is_src)
        def _():
            for way in range(1, 4):
                left(16, bc_send.at[it, way])

            @pl.when(far_plane == 1)
            def _():
                left(16, bc_send.at[it, 0])

    def f_left(pieces, sem):
        arrived(fr.at[pl.ds(0, pieces * f_rows)], sem)

    for way, d in ((RIGHT, d_right), (LEFT, d_left)):
        @pl.when(d < ZN - 1)
        def _(way=way):
            f_left(FP, f_send.at[way])

    @pl.when(jnp.logical_and(is_seed, far_plane == 1))
    def _():
        f_left(2 * FP, f_send.at[2])

    f_left(2 * FP, f_send.at[3])
    arrived(block(x, yl), b_send.at[0])
    arrived(pair(x), b_send.at[1])
    arrived(pair(x), b_send.at[2])
    arrived(block(x, yl), b_send.at[3])
    arrived(block(x, yl), b_send.at[4])
    arrived(bs.at[pl.ds(core * 8, 8)], b_send.at[5])


def body(amplitudes, coulomb, fit_ov, fit_vv, eps_occ, eps_vir):
    occ_local, occ_other, virtual, _ = amplitudes.shape
    aux = fit_ov.shape[0]
    side = occ_local * virtual
    sub = side // (4 * ZN)
    fit = fit_ov.reshape(aux, occ_other * virtual)
    batch = fit_vv.shape[0] * lax.axis_size("row")
    vmem = pl.BlockSpec(memory_space=pltpu.VMEM)
    dma = pltpu.SemaphoreType.DMA
    return pl.pallas_call(
        kernel,
        out_shape=jax.ShapeDtypeStruct(amplitudes.shape, BF16),
        in_specs=[pl.BlockSpec(memory_space=pltpu.SMEM)] + [vmem] * 5,
        out_specs=vmem,
        scratch_shapes=[
            pltpu.VMEM((side, occ_other * virtual), BF16),
            pltpu.VMEM((ITERS, side, aux), BF16),
            pltpu.VMEM((ITERS, 2, 4, 2, sub, aux), BF16),
            pltpu.VMEM((ITERS, 2, 4, sub, aux), BF16),
            pltpu.VMEM((ITERS, ZN, sub, aux), BF16),
            pltpu.VMEM((ITERS, 2, sub, aux), BF16),
            pltpu.VMEM((ITERS, 2, sub, aux), BF16),
            pltpu.VMEM((ITERS, 2, side, aux), BF16),
            pltpu.VMEM((aux, side), BF16),
            pltpu.VMEM((batch, virtual, virtual), BF16),
            pltpu.VMEM((occ_local * occ_other, virtual, virtual), F32),
            pltpu.VMEM((4, 4 * virtual, virtual), BF16),
            pltpu.VMEM((virtual, virtual), F32),
            dma((ITERS, 2, 4, 2)),
            dma((ITERS, 2, 4)),
            dma((ITERS, 3, ZN)),
            dma((ITERS, 2, 4, 2)),
            dma((ITERS, 2, 4)),
            dma((ITERS, 4 * ZN)),
            dma((2, 2, FP)),
            dma((6,)),
            dma((ITERS,)),
            dma((ITERS,)),
            dma((ITERS,)),
            dma((ITERS, 7)),
            dma((4,)),
            dma((6,)),
            dma,
        ],
        compiler_params=pltpu.CompilerParams(
            collective_id=0, has_side_effects=True, vmem_limit_bytes=60 * 2**20
        ),
        name="sweeps",
    )(eps_occ, amplitudes, coulomb, fit, fit_vv, eps_vir[None, :])


def solution(mesh):
    in_specs = (
        P("row", "col", None, None),
        P("row", "col", None, None),
        P(None, "col", None),
        P("row", None, None),
        P(),
        P(),
    )
    out_specs = P("row", "col", None, None)
    return jax.shard_map(body, mesh=mesh, in_specs=in_specs, out_specs=out_specs, check_vma=False)
```

```python
import jax
import jax.numpy as jnp
from jax import lax
from jax.experimental import pallas as pl
from jax.experimental.pallas import tpu as pltpu
from jax.sharding import PartitionSpec as P

ITERS = 2
MESH = pl.DeviceIdType.MESH
F32 = jnp.float32
BF16 = jnp.bfloat16

ZN = 8
XN = 4
RIGHT, LEFT = 0, 1
F_OVER = 8
FP = 8


def nn(a, b):
    return jnp.dot(a, b, preferred_element_type=F32)


def nt(a, b):
    return lax.dot_general(a, b, (((1,), (1,)), ((), ())), preferred_element_type=F32)


def tt(a, b):
    return lax.dot_general(a, b, (((0,), (1,)), ((), ())), preferred_element_type=F32)


def kernel(eps, amp, coul, fit, own_b, ev_row, out,
           t2, part, rsa, rsb, yfirst, yv, yr, pp, fr, bs, acc, con, ev_col,
           rsa_sem, rsb_sem, y_sem, aga_sem, agb_sem, bc_sem, f_sem, b_sem,
           rs_send, y_send, ag_send, bc_send, f_send, b_send, local_sem):
    row = lax.axis_index("row")
    col = lax.axis_index("col")
    core = lax.rem(row, 2)
    x = lax.rem(row // 2, XN)
    yl = row // (2 * XN)
    z = lax.rem(col, ZN)
    yh = col // ZN

    def dev(yl_, x_, core_, yh_, z_):
        return (yl_ * (2 * XN) + x_ * 2 + core_, yh_ * ZN + z_)

    z_next = dev(yl, x, core, yh, lax.rem(z + 1, ZN))
    z_prev = dev(yl, x, core, yh, lax.rem(z + ZN - 1, ZN))
    x_next = dev(yl, lax.rem(x + 1, XN), core, yh, z)
    x_prev = dev(yl, lax.rem(x + XN - 1, XN), core, yh, z)
    y_far = dev(yl, x, core, 1 - yh, z)
    y_near = dev(1 - yl, x, core, yh, z)
    y_both = dev(1 - yl, x, core, 1 - yh, z)
    mate = dev(yl, x, 1 - core, yh, z)

    z_next2 = dev(yl, x, core, yh, lax.rem(z + 2, ZN))
    z_prev2 = dev(yl, x, core, yh, lax.rem(z + ZN - 2, ZN))
    far_plane = (yl != yh).astype(jnp.int32)

    def plane_peer(flip, shift):
        yl_ = jnp.where(flip == 1, 1 - yl, yl)
        yh_ = jnp.where(flip == 1, 1 - yh, yh)
        return dev(yl_, lax.rem(x + shift, XN), core, yh_, z)

    barrier = pltpu.get_barrier_semaphore()
    peers = [z_next, z_prev, z_next2, z_prev2, y_far, y_near, mate]
    peers += [plane_peer(0, shift) for shift in range(1, XN)] + [plane_peer(1, shift) for shift in range(XN)]
    for peer in peers:
        pl.semaphore_signal(barrier, inc=1, device_id=peer, device_id_type=MESH)
    pl.semaphore_wait(barrier, len(peers))

    def send(src, dst, send_sem, recv_sem, peer):
        pltpu.make_async_remote_copy(
            src_ref=src, dst_ref=dst, send_sem=send_sem, recv_sem=recv_sem,
            device_id=peer, device_id_type=MESH,
        ).start()

    def arrived(ref, sem):
        pltpu.make_async_copy(ref, ref, sem).wait()

    virtual = amp.shape[2]
    side = part.shape[1]
    sub = side // (4 * ZN)
    f_rows = fit.shape[0] // (4 * FP)
    ring = {RIGHT: z_next, LEFT: z_prev}
    ring2 = {RIGHT: z_next2, LEFT: z_prev2}
    toward = {RIGHT: 1, LEFT: ZN - 1}
    even = lax.rem(z, 2) == 0
    b_long = {RIGHT: even, LEFT: jnp.logical_not(even)}

    def a_rows(o, s):
        return pl.ds(pl.multiple_of((o * 2 + s) * sub, sub), sub)

    def b_rows(v, o):
        return pl.ds(pl.multiple_of(side // 2 + v * (side // 4) + o * sub, sub), sub)

    z_seed = 2 * x + core
    d_right = lax.rem(z + ZN - z_seed, ZN)
    d_left = lax.rem(z_seed + ZN - z, ZN)
    is_seed = z == z_seed

    def f_ref(ref, v, way, p):
        return ref.at[pl.ds(pl.multiple_of(((v * 2 + way) * FP + p) * f_rows, f_rows), f_rows)]

    @pl.when(jnp.logical_and(is_seed, far_plane == 0))
    def _():
        ref = pl.ds(pl.multiple_of(yh * 2 * FP * f_rows, f_rows), 2 * FP * f_rows)
        own = pltpu.make_async_copy(fit.at[ref], fr.at[ref], local_sem)
        own.start()
        own.wait()

    def f_seed():
        @pl.when(jnp.logical_and(is_seed, far_plane == 1))
        def _():
            for p in range(FP):
                for way in (RIGHT, LEFT):
                    send(f_ref(fit, 1 - yh, way, p), f_ref(fr, 1 - yh, way, p), f_send.at[2], f_sem.at[0, way, p], y_both)

    def f_delay(d):
        return 2 * d + 2 * far_plane

    def f_over(k):
        for p in range(FP):
            for way, d in ((RIGHT, d_right), (LEFT, d_left)):
                @pl.when(k == jnp.maximum(p + f_delay(d), F_OVER))
                def _(way=way, p=p):
                    ref = f_ref(fr, yh, way, p)
                    send(ref, ref, f_send.at[3], f_sem.at[1, way, p], y_far)

    def f_step(k):
        for way, d in ((RIGHT, d_right), (LEFT, d_left)):
            p = k - f_delay(d)

            @pl.when(jnp.logical_and(p >= 0, p < FP))
            def _(way=way, d=d, p=p):
                ref = f_ref(fr, yh, way, p)

                @pl.when(jnp.logical_or(d > 0, far_plane == 1))
                def _():
                    arrived(ref, f_sem.at[0, way, p])

                @pl.when(d < ZN - 1)
                def _():
                    send(ref, ref, f_send.at[way], f_sem.at[0, way, p], ring[way])

    def pair(x_):
        return bs.at[pl.ds(core * 8 + x_ * 2, 2)]

    def block(x_, yl_):
        return bs.at[pl.ds(core * 8 + x_ * 2 + yl_, 1)]

    x_up = lax.rem(x + 1, XN)
    x_down = lax.rem(x + XN - 1, XN)
    x_two = lax.rem(x + 2, XN)

    def b_step(k):
        @pl.when(k == 0)
        def _():
            send(own_b, block(x, yl), b_send.at[0], b_sem.at[0], y_near)
            own = pltpu.make_async_copy(own_b, block(x, yl), local_sem)
            own.start()
            own.wait()

        @pl.when(k == 2)
        def _():
            arrived(block(x, 1 - yl), b_sem.at[0])
            send(pair(x), pair(x), b_send.at[1], b_sem.at[1], x_next)
            send(pair(x), pair(x), b_send.at[2], b_sem.at[2], x_prev)

        @pl.when(k == 4)
        def _():
            arrived(pair(x_down), b_sem.at[1])
            arrived(pair(x_up), b_sem.at[2])
            send(block(x_down, yl), block(x_down, yl), b_send.at[3], b_sem.at[3], x_next)
            send(block(x_up, 1 - yl), block(x_up, 1 - yl), b_send.at[4], b_sem.at[4], x_prev)

        @pl.when(k == 6)
        def _():
            arrived(block(x_two, yl), b_sem.at[3])
            arrived(block(x_two, 1 - yl), b_sem.at[4])
            lane = bs.at[pl.ds(core * 8, 8)]
            send(lane, lane, b_send.at[5], b_sem.at[5], mate)

        @pl.when(k == 8)
        def _():
            other = bs.at[pl.ds((1 - core) * 8, 8)]
            arrived(other, b_sem.at[5])

    dx = lax.rem(x + XN - z // 2, XN)
    on_lane = core == lax.rem(z, 2)
    is_src = jnp.logical_and(on_lane, dx == 0)
    is_near_src = jnp.logical_and(is_src, far_plane == 0)
    sel = 1 - is_near_src.astype(jnp.int32)

    for i in range(2):
        for j in range(2):
            t2[i * virtual:(i + 1) * virtual, j * virtual:(j + 1) * virtual] = amp[i, j]
    ev_col[...] = jnp.broadcast_to(ev_row[...], (virtual, virtual)).T

    @pl.loop(0, ITERS)
    def _(it):
        first = it == 0

        quarter = side // 4
        theirs = pl.ds(pl.multiple_of(side // 2 + (1 - yh) * quarter, quarter), quarter)
        mine = pl.ds(pl.multiple_of(side // 2 + yh * quarter, quarter), quarter)
        part[it, theirs, :] = nt(t2[theirs, :], fit[...]).astype(BF16)
        for u in (4, 3, 5, 2, 6, 1, 7, 0):
            o = lax.rem(z + u, ZN)
            send(part.at[it, b_rows(1 - yh, o)], yfirst.at[it, o], y_send.at[it], y_sem.at[it, 0, o], y_far)
        @pl.when(first)
        def _():
            f_seed()

        part[it, 0:side // 2, :] = nt(t2[0:side // 2, :], fit[...]).astype(BF16)

        def there(way, steps):
            return lax.rem(z + steps * toward[way], ZN)

        def add_a(at, way, slot, s):
            ref = rsa.at[it, way, slot, s]
            arrived(ref, rsa_sem.at[it, way, slot, s])
            return ref[...].astype(F32)

        def send_a(at, way, slot, s, peer):
            send(part.at[it, at], rsa.at[it, way, slot, s], rs_send.at[it], rsa_sem.at[it, way, slot, s], peer)

        def add_b(way, slot):
            ref = rsb.at[it, way, slot]
            arrived(ref, rsb_sem.at[it, way, slot])
            return ref[...].astype(F32)

        def send_b(at, way, slot, peer):
            send(part.at[it, at], rsb.at[it, way, slot], rs_send.at[it], rsb_sem.at[it, way, slot], peer)

        def both_halves(at, o):
            arrived(yfirst.at[it, o], y_sem.at[it, 0, o])
            return part[it, at, :].astype(F32) + yfirst[it, o].astype(F32)

        for k in range(4):
            def round_a(k):
                for s in range(2):
                    for way in (RIGHT, LEFT):
                        long = s == way
                        if k == 0:
                            if long:
                                send_a(a_rows(there(way, 4), s), way, 0, s, ring2[way])
                            send_a(a_rows(there(way, 3), s), way, 1, s, ring[way])
                        elif k < 3:
                            at = a_rows(there(way, 3 - k), s)
                            total = part[it, at, :].astype(F32) + add_a(at, way, k, s)
                            if k == 1 and long:
                                total = total + add_a(at, way, 0, s)
                            part[it, at, :] = total.astype(BF16)
                            send_a(at, way, k + 1, s, ring[way])
            def round_b(k):
                for way in (RIGHT, LEFT):
                    if k == 1:
                        @pl.when(b_long[way])
                        def _(way=way):
                            o = there(way, 4)
                            at = b_rows(yh, o)
                            part[it, at, :] = both_halves(at, o).astype(BF16)
                            send_b(at, way, 0, ring2[way])

                        o = there(way, 3)
                        at = b_rows(yh, o)
                        part[it, at, :] = both_halves(at, o).astype(BF16)
                        send_b(at, way, 1, ring[way])
                    elif k > 1:
                        o = there(way, 4 - k)
                        at = b_rows(yh, o)
                        total = both_halves(at, o) + add_b(way, k - 1)
                        part[it, at, :] = total.astype(BF16)
                        if k == 2:
                            @pl.when(b_long[way])
                            def _(way=way, at=at):
                                part[it, at, :] = (part[it, at, :].astype(F32) + add_b(way, 0)).astype(BF16)
                        send_b(at, way, k, ring[way])

            if k == 0:
                round_a(k)
            else:
                round_b(k)

            @pl.when(first)
            def _(k=k):
                f_step(2 * k)

            if k == 0:
                part[it, mine, :] = nt(t2[mine, :], fit[...]).astype(BF16)
                acc[...] = jnp.zeros_like(acc)
            if k > 0:
                round_a(k)

            @pl.when(first)
            def _(k=k):
                f_step(2 * k + 1)
                b_step(k)

        for s in range(2):
            at = a_rows(z, s)
            for way in (RIGHT, LEFT):
                arrived(rsa.at[it, way, 3, s], rsa_sem.at[it, way, 3, s])
            yv[it, s] = (
                part[it, at, :].astype(F32)
                + rsa[it, RIGHT, 3, s].astype(F32)
                + rsa[it, LEFT, 3, s].astype(F32)
            ).astype(BF16)
            send(yv.at[it, s], yr.at[it, s], y_send.at[it], y_sem.at[it, 1, s], y_far)

        @pl.when(first)
        def _():
            f_step(8)
            f_over(8)

        def own_sends(ref, sems):
            for way in (RIGHT, LEFT):
                send(ref, ref, ag_send.at[it], sems[way], ring[way])

        def to_far(ref, o):
            send(ref, ref, y_send.at[it], y_sem.at[it, 2, o], y_far)

        at = b_rows(yh, z)
        arrived(yfirst.at[it, z], y_sem.at[it, 0, z])
        for way in (RIGHT, LEFT):
            arrived(rsb.at[it, way, 3], rsb_sem.at[it, way, 3])
        pp[it, 0, at, :] = (
            part[it, at, :].astype(F32) + yfirst[it, z].astype(F32)
            + rsb[it, RIGHT, 3].astype(F32) + rsb[it, LEFT, 3].astype(F32)
        ).astype(BF16)
        own_sends(pp.at[it, 0, at], [agb_sem.at[it, way, 0] for way in (RIGHT, LEFT)])
        to_far(pp.at[it, 0, at], z)
        for s in range(2):
            at = a_rows(z, s)
            arrived(yr.at[it, s], y_sem.at[it, 1, s])
            pp[it, 0, at, :] = (yv[it, s].astype(F32) + yr[it, s].astype(F32)).astype(BF16)
            own_sends(pp.at[it, 0, at], [aga_sem.at[it, way, 0, s] for way in (RIGHT, LEFT)])

        def sent_on(ref, way, n, long, sems):
            @pl.when(n < 3)
            def _():
                send(ref, ref, ag_send.at[it], sems(n), ring[way])

            @pl.when(jnp.logical_and(n == 2, long))
            def _():
                send(ref, ref, ag_send.at[it], sems(3), ring2[way])

        def group(m, act):
            act(lax.rem(z + ZN - m, ZN))

            @pl.when(m >= 1)
            def _():
                act(lax.rem(z + m, ZN))

            @pl.when(m == 3)
            def _():
                act(lax.rem(z + 4, ZN))

        def relay(o):
            for at, index in (
                (a_rows(o, 1 - far_plane), (1 - far_plane) * 16 + o),
                (b_rows(1 - yl, o), (1 - far_plane) * 16 + 8 + o),
            ):
                ref, sem = pp.at[it, 1, at], bc_sem.at[it, index]
                arrived(ref, sem)
                send(ref, ref, bc_send.at[it, 5], sem, mate)

        @pl.loop(0, 6)
        def _(n):
            @pl.when(jnp.logical_and(n >= 1, n <= 3))
            def _():
                for way in (RIGHT, LEFT):
                    o = lax.rem(z + n * toward[1 - way], ZN)
                    ref = pp.at[it, 0, b_rows(yh, o)]
                    arrived(ref, agb_sem.at[it, way, n - 1])
                    sent_on(ref, way, n, b_long[way], lambda h, way=way: agb_sem.at[it, way, h])
                    to_far(ref, o)
                for s in range(2):
                    for way in (RIGHT, LEFT):
                        o = lax.rem(z + n * toward[1 - way], ZN)
                        ref = pp.at[it, 0, a_rows(o, s)]
                        arrived(ref, aga_sem.at[it, way, n - 1, s])
                        sent_on(ref, way, n, s == way, lambda h, way=way, s=s: aga_sem.at[it, way, h, s])

            @pl.when(n == 3)
            def _():
                o = lax.rem(z + 4, ZN)
                for way in (RIGHT, LEFT):
                    @pl.when(b_long[way])
                    def _(way=way):
                        ref = pp.at[it, 0, b_rows(yh, o)]
                        arrived(ref, agb_sem.at[it, way, 3])
                        to_far(ref, o)
                    arrived(pp.at[it, 0, a_rows(o, way)], aga_sem.at[it, way, 3, way])

            @pl.when(first)
            def _():
                f_step(9 + 2 * n)
                f_over(9 + 2 * n)

            @pl.when(jnp.logical_and(is_src, n <= 3))
            def _():
                def act(o):
                    for at, index in (
                        (a_rows(o, far_plane), far_plane * 16 + o),
                        (b_rows(yh, o), far_plane * 16 + 8 + o),
                    ):
                        src, dst, sem = pp.at[it, 0, at], pp.at[it, 1, at], bc_sem.at[it, index]
                        for shift in range(1, XN):
                            send(src, dst, bc_send.at[it, shift], sem, plane_peer(far_plane, shift))

                        @pl.when(far_plane == 1)
                        def _():
                            send(src, dst, bc_send.at[it, 0], sem, plane_peer(1, 0))

                group(n, act)

            m = n - 2 * sel

            @pl.when(jnp.logical_and(on_lane, jnp.logical_and(m >= 0, m <= 3)))
            def _():
                def act(o):
                    for at, index in (
                        (a_rows(o, far_plane), far_plane * 16 + o),
                        (b_rows(yl, o), far_plane * 16 + 8 + o),
                    ):
                        src, dst, sem = pp.at[it, sel, at], pp.at[it, 1, at], bc_sem.at[it, index]

                        @pl.when(sel == 1)
                        def _():
                            arrived(dst, sem)

                        send(src, dst, bc_send.at[it, 4], sem, y_near)
                        send(src, dst, bc_send.at[it, 6], sem, mate)

                group(m, act)

            @pl.when(jnp.logical_and(on_lane, n >= 4))
            def _():
                @pl.loop(n - 4, 2 * n - 7)
                def _(m):
                    group(m, relay)

            @pl.when(first)
            def _():
                f_step(10 + 2 * n)
                f_over(10 + 2 * n)
                b_step(n + 4)

            @pl.when(n >= 2)
            def _():
                start = lax.rem(core * 8 + (n - 2) * 4, 16)
                bb = bs[pl.ds(start, 4)].reshape(4 * virtual, virtual)
                for p in range(4):
                    i, j = p // 2, p % 2
                    con[p] = nn(
                        bb, t2[i * virtual:(i + 1) * virtual, j * virtual:(j + 1) * virtual]
                    ).astype(BF16)
                for p in range(4):
                    total = acc[p]
                    for k in range(4):
                        total = total + nt(con[p, k * virtual:(k + 1) * virtual, :], bb[k * virtual:(k + 1) * virtual])
                    acc[p] = total

            @pl.when(n == 5)
            def _():
                for o in range(ZN):
                    arrived(pp.at[it, 0, b_rows(1 - yh, o)], y_sem.at[it, 2, o])

            @pl.when(n >= 4)
            def _():
                i = n - 4
                term = nn(pp[it, 0, pl.ds(pl.multiple_of(i * virtual, virtual), virtual), :], fit[...])
                for j in range(2):
                    acc[2 * i + j] += term[:, j * virtual:(j + 1) * virtual]

        @pl.when(first)
        def _():
            @pl.loop(21, 26)
            def _(k):
                f_step(k)
                f_over(k)

            for way in (RIGHT, LEFT):
                for p in range(FP):
                    arrived(f_ref(fr, 1 - yh, way, p), f_sem.at[1, way, p])

        @pl.when(on_lane)
        def _():
            group(3, relay)

        for path in range(2):
            @pl.when(jnp.logical_not(on_lane))
            def _(path=path):
                for o in range(ZN):
                    arrived(pp.at[it, 1, a_rows(o, path)], bc_sem.at[it, path * 16 + o])
                    half = yh if path == 0 else 1 - yh
                    arrived(pp.at[it, 1, b_rows(half, o)], bc_sem.at[it, path * 16 + 8 + o])

        for i in range(2):
            term = tt(fr[:, i * virtual:(i + 1) * virtual], pp[it, sel])
            for j in range(2):
                total = coul[i, j].astype(F32) + acc[2 * i + j] + term[:, j * virtual:(j + 1) * virtual]
                denominator = (eps[row * 2 + i] + eps[col * 2 + j]) - ev_col[...] - ev_row[...]
                updated = (total / denominator).astype(BF16)
                t2[i * virtual:(i + 1) * virtual, j * virtual:(j + 1) * virtual] = updated
                out[i, j] = updated

        def left(pieces, sem):
            arrived(part.at[it, pl.ds(0, pieces * sub)], sem)

        left(21, rs_send.at[it])
        left(21, ag_send.at[it])
        left(18, y_send.at[it])

        @pl.when(on_lane)
        def _():
            for way in range(4, 7):
                left(16, bc_send.at[it, way])

        @pl.when(is_src)
        def _():
            for way in range(1, 4):
                left(16, bc_send.at[it, way])

            @pl.when(far_plane == 1)
            def _():
                left(16, bc_send.at[it, 0])

    def f_left(pieces, sem):
        arrived(fr.at[pl.ds(0, pieces * f_rows)], sem)

    for way, d in ((RIGHT, d_right), (LEFT, d_left)):
        @pl.when(d < ZN - 1)
        def _(way=way):
            f_left(FP, f_send.at[way])

    @pl.when(jnp.logical_and(is_seed, far_plane == 1))
    def _():
        f_left(2 * FP, f_send.at[2])

    f_left(2 * FP, f_send.at[3])
    arrived(block(x, yl), b_send.at[0])
    arrived(pair(x), b_send.at[1])
    arrived(pair(x), b_send.at[2])
    arrived(block(x, yl), b_send.at[3])
    arrived(block(x, yl), b_send.at[4])
    arrived(bs.at[pl.ds(core * 8, 8)], b_send.at[5])


def body(amplitudes, coulomb, fit_ov, fit_vv, eps_occ, eps_vir):
    occ_local, occ_other, virtual, _ = amplitudes.shape
    aux = fit_ov.shape[0]
    side = occ_local * virtual
    sub = side // (4 * ZN)
    fit = fit_ov.reshape(aux, occ_other * virtual)
    batch = fit_vv.shape[0] * lax.axis_size("row")
    vmem = pl.BlockSpec(memory_space=pltpu.VMEM)
    dma = pltpu.SemaphoreType.DMA
    return pl.pallas_call(
        kernel,
        out_shape=jax.ShapeDtypeStruct(amplitudes.shape, BF16),
        in_specs=[pl.BlockSpec(memory_space=pltpu.SMEM)] + [vmem] * 5,
        out_specs=vmem,
        scratch_shapes=[
            pltpu.VMEM((side, occ_other * virtual), BF16),
            pltpu.VMEM((ITERS, side, aux), BF16),
            pltpu.VMEM((ITERS, 2, 4, 2, sub, aux), BF16),
            pltpu.VMEM((ITERS, 2, 4, sub, aux), BF16),
            pltpu.VMEM((ITERS, ZN, sub, aux), BF16),
            pltpu.VMEM((ITERS, 2, sub, aux), BF16),
            pltpu.VMEM((ITERS, 2, sub, aux), BF16),
            pltpu.VMEM((ITERS, 2, side, aux), BF16),
            pltpu.VMEM((aux, side), BF16),
            pltpu.VMEM((batch, virtual, virtual), BF16),
            pltpu.VMEM((occ_local * occ_other, virtual, virtual), F32),
            pltpu.VMEM((4, 4 * virtual, virtual), BF16),
            pltpu.VMEM((virtual, virtual), F32),
            dma((ITERS, 2, 4, 2)),
            dma((ITERS, 2, 4)),
            dma((ITERS, 3, ZN)),
            dma((ITERS, 2, 4, 2)),
            dma((ITERS, 2, 4)),
            dma((ITERS, 4 * ZN)),
            dma((2, 2, FP)),
            dma((6,)),
            dma((ITERS,)),
            dma((ITERS,)),
            dma((ITERS,)),
            dma((ITERS, 7)),
            dma((4,)),
            dma((6,)),
            dma,
        ],
        compiler_params=pltpu.CompilerParams(
            collective_id=0, has_side_effects=True, vmem_limit_bytes=60 * 2**20
        ),
        name="sweeps",
    )(eps_occ, amplitudes, coulomb, fit, fit_vv, eps_vir[None, :])


def solution(mesh):
    in_specs = (
        P("row", "col", None, None),
        P("row", "col", None, None),
        P(None, "col", None),
        P("row", None, None),
        P(),
        P(),
    )
    out_specs = P("row", "col", None, None)
    return jax.shard_map(body, mesh=mesh, in_specs=in_specs, out_specs=out_specs, check_vma=False)
```

```python
import jax
import jax.numpy as jnp
from jax import lax
from jax.experimental import pallas as pl
from jax.experimental.pallas import tpu as pltpu
from jax.sharding import PartitionSpec as P

ITERS = 2
MESH = pl.DeviceIdType.MESH
F32 = jnp.float32
BF16 = jnp.bfloat16

ZN = 8
XN = 4
RIGHT, LEFT = 0, 1
F_OVER = 8
FP = 8


def nn(a, b):
    return jnp.dot(a, b, preferred_element_type=F32)


def nt(a, b):
    return lax.dot_general(a, b, (((1,), (1,)), ((), ())), preferred_element_type=F32)


def tt(a, b):
    return lax.dot_general(a, b, (((0,), (1,)), ((), ())), preferred_element_type=F32)


def kernel(eps, amp, coul_hbm, fit, own_b, ev_row, out,
           t2, part, rsa, rsb, yfirst, yv, yr, pp, fr, bs, acc, con, ev_col,
           rsa_sem, rsb_sem, y_sem, aga_sem, agb_sem, bc_sem, f_sem, b_sem,
           rs_send, y_send, ag_send, bc_send, f_send, b_send, local_sem, coul, coul_sem):
    row = lax.axis_index("row")
    col = lax.axis_index("col")
    core = lax.rem(row, 2)
    x = lax.rem(row // 2, XN)
    yl = row // (2 * XN)
    z = lax.rem(col, ZN)
    yh = col // ZN

    def dev(yl_, x_, core_, yh_, z_):
        return (yl_ * (2 * XN) + x_ * 2 + core_, yh_ * ZN + z_)

    z_next = dev(yl, x, core, yh, lax.rem(z + 1, ZN))
    z_prev = dev(yl, x, core, yh, lax.rem(z + ZN - 1, ZN))
    x_next = dev(yl, lax.rem(x + 1, XN), core, yh, z)
    x_prev = dev(yl, lax.rem(x + XN - 1, XN), core, yh, z)
    y_far = dev(yl, x, core, 1 - yh, z)
    y_near = dev(1 - yl, x, core, yh, z)
    y_both = dev(1 - yl, x, core, 1 - yh, z)
    mate = dev(yl, x, 1 - core, yh, z)

    z_next2 = dev(yl, x, core, yh, lax.rem(z + 2, ZN))
    z_prev2 = dev(yl, x, core, yh, lax.rem(z + ZN - 2, ZN))
    far_plane = (yl != yh).astype(jnp.int32)

    def plane_peer(flip, shift):
        yl_ = jnp.where(flip == 1, 1 - yl, yl)
        yh_ = jnp.where(flip == 1, 1 - yh, yh)
        return dev(yl_, lax.rem(x + shift, XN), core, yh_, z)

    barrier = pltpu.get_barrier_semaphore()
    peers = [z_next, z_prev, z_next2, z_prev2, y_far, y_near, mate]
    peers += [plane_peer(0, shift) for shift in range(1, XN)] + [plane_peer(1, shift) for shift in range(XN)]
    for peer in peers:
        pl.semaphore_signal(barrier, inc=1, device_id=peer, device_id_type=MESH)
    pl.semaphore_wait(barrier, len(peers))

    def send(src, dst, send_sem, recv_sem, peer):
        pltpu.make_async_remote_copy(
            src_ref=src, dst_ref=dst, send_sem=send_sem, recv_sem=recv_sem,
            device_id=peer, device_id_type=MESH,
        ).start()

    def arrived(ref, sem):
        pltpu.make_async_copy(ref, ref, sem).wait()

    exchange = pltpu.make_async_copy(coul_hbm, coul, coul_sem)
    exchange.start()
    virtual = amp.shape[2]
    side = part.shape[1]
    sub = side // (4 * ZN)
    f_rows = fit.shape[0] // (4 * FP)
    ring = {RIGHT: z_next, LEFT: z_prev}
    ring2 = {RIGHT: z_next2, LEFT: z_prev2}
    toward = {RIGHT: 1, LEFT: ZN - 1}
    even = lax.rem(z, 2) == 0
    b_long = {RIGHT: even, LEFT: jnp.logical_not(even)}

    def a_rows(o, s):
        return pl.ds(pl.multiple_of((o * 2 + s) * sub, sub), sub)

    def b_rows(v, o):
        return pl.ds(pl.multiple_of(side // 2 + v * (side // 4) + o * sub, sub), sub)

    z_seed = 2 * x + core
    d_right = lax.rem(z + ZN - z_seed, ZN)
    d_left = lax.rem(z_seed + ZN - z, ZN)
    is_seed = z == z_seed

    def f_ref(ref, v, way, p):
        return ref.at[pl.ds(pl.multiple_of(((v * 2 + way) * FP + p) * f_rows, f_rows), f_rows)]

    @pl.when(jnp.logical_and(is_seed, far_plane == 0))
    def _():
        ref = pl.ds(pl.multiple_of(yh * 2 * FP * f_rows, f_rows), 2 * FP * f_rows)
        own = pltpu.make_async_copy(fit.at[ref], fr.at[ref], local_sem)
        own.start()
        own.wait()

    def f_seed():
        @pl.when(jnp.logical_and(is_seed, far_plane == 1))
        def _():
            for p in range(FP):
                for way in (RIGHT, LEFT):
                    send(f_ref(fit, 1 - yh, way, p), f_ref(fr, 1 - yh, way, p), f_send.at[2], f_sem.at[0, way, p], y_both)

    def f_delay(d):
        return 2 * d + 2 * far_plane

    def f_over(k):
        for p in range(FP):
            for way, d in ((RIGHT, d_right), (LEFT, d_left)):
                @pl.when(k == jnp.maximum(p + f_delay(d), F_OVER))
                def _(way=way, p=p):
                    ref = f_ref(fr, yh, way, p)
                    send(ref, ref, f_send.at[3], f_sem.at[1, way, p], y_far)

    def f_step(k):
        for way, d in ((RIGHT, d_right), (LEFT, d_left)):
            p = k - f_delay(d)

            @pl.when(jnp.logical_and(p >= 0, p < FP))
            def _(way=way, d=d, p=p):
                ref = f_ref(fr, yh, way, p)

                @pl.when(jnp.logical_or(d > 0, far_plane == 1))
                def _():
                    arrived(ref, f_sem.at[0, way, p])

                @pl.when(d < ZN - 1)
                def _():
                    send(ref, ref, f_send.at[way], f_sem.at[0, way, p], ring[way])

    def pair(x_):
        return bs.at[pl.ds(core * 8 + x_ * 2, 2)]

    def block(x_, yl_):
        return bs.at[pl.ds(core * 8 + x_ * 2 + yl_, 1)]

    x_up = lax.rem(x + 1, XN)
    x_down = lax.rem(x + XN - 1, XN)
    x_two = lax.rem(x + 2, XN)

    def b_step(k):
        @pl.when(k == 0)
        def _():
            send(own_b, block(x, yl), b_send.at[0], b_sem.at[0], y_near)
            own = pltpu.make_async_copy(own_b, block(x, yl), local_sem)
            own.start()
            own.wait()

        @pl.when(k == 2)
        def _():
            arrived(block(x, 1 - yl), b_sem.at[0])
            send(pair(x), pair(x), b_send.at[1], b_sem.at[1], x_next)
            send(pair(x), pair(x), b_send.at[2], b_sem.at[2], x_prev)

        @pl.when(k == 4)
        def _():
            arrived(pair(x_down), b_sem.at[1])
            arrived(pair(x_up), b_sem.at[2])
            send(block(x_down, yl), block(x_down, yl), b_send.at[3], b_sem.at[3], x_next)
            send(block(x_up, 1 - yl), block(x_up, 1 - yl), b_send.at[4], b_sem.at[4], x_prev)

        @pl.when(k == 6)
        def _():
            arrived(block(x_two, yl), b_sem.at[3])
            arrived(block(x_two, 1 - yl), b_sem.at[4])
            lane = bs.at[pl.ds(core * 8, 8)]
            send(lane, lane, b_send.at[5], b_sem.at[5], mate)

        @pl.when(k == 8)
        def _():
            other = bs.at[pl.ds((1 - core) * 8, 8)]
            arrived(other, b_sem.at[5])

    dx = lax.rem(x + XN - z // 2, XN)
    on_lane = core == lax.rem(z, 2)
    is_src = jnp.logical_and(on_lane, dx == 0)
    is_near_src = jnp.logical_and(is_src, far_plane == 0)
    sel = 1 - is_near_src.astype(jnp.int32)

    for i in range(2):
        for j in range(2):
            t2[i * virtual:(i + 1) * virtual, j * virtual:(j + 1) * virtual] = amp[i, j]
    ev_col[...] = jnp.broadcast_to(ev_row[...], (virtual, virtual)).T

    @pl.loop(0, ITERS)
    def _(it):
        first = it == 0

        quarter = side // 4
        theirs = pl.ds(pl.multiple_of(side // 2 + (1 - yh) * quarter, quarter), quarter)
        mine = pl.ds(pl.multiple_of(side // 2 + yh * quarter, quarter), quarter)
        part[it, theirs, :] = nt(t2[theirs, :], fit[...]).astype(BF16)
        for u in (4, 3, 5, 2, 6, 1, 7, 0):
            o = lax.rem(z + u, ZN)
            send(part.at[it, b_rows(1 - yh, o)], yfirst.at[it, o], y_send.at[it], y_sem.at[it, 0, o], y_far)
        @pl.when(first)
        def _():
            f_seed()

        part[it, 0:side // 2, :] = nt(t2[0:side // 2, :], fit[...]).astype(BF16)

        def there(way, steps):
            return lax.rem(z + steps * toward[way], ZN)

        def add_a(at, way, slot, s):
            ref = rsa.at[it, way, slot, s]
            arrived(ref, rsa_sem.at[it, way, slot, s])
            return ref[...].astype(F32)

        def send_a(at, way, slot, s, peer):
            send(part.at[it, at], rsa.at[it, way, slot, s], rs_send.at[it], rsa_sem.at[it, way, slot, s], peer)

        def add_b(way, slot):
            ref = rsb.at[it, way, slot]
            arrived(ref, rsb_sem.at[it, way, slot])
            return ref[...].astype(F32)

        def send_b(at, way, slot, peer):
            send(part.at[it, at], rsb.at[it, way, slot], rs_send.at[it], rsb_sem.at[it, way, slot], peer)

        def both_halves(at, o):
            arrived(yfirst.at[it, o], y_sem.at[it, 0, o])
            return part[it, at, :].astype(F32) + yfirst[it, o].astype(F32)

        for k in range(4):
            def round_a(k):
                for s in range(2):
                    for way in (RIGHT, LEFT):
                        long = s == way
                        if k == 0:
                            if long:
                                send_a(a_rows(there(way, 4), s), way, 0, s, ring2[way])
                            send_a(a_rows(there(way, 3), s), way, 1, s, ring[way])
                        elif k < 3:
                            at = a_rows(there(way, 3 - k), s)
                            total = part[it, at, :].astype(F32) + add_a(at, way, k, s)
                            if k == 1 and long:
                                total = total + add_a(at, way, 0, s)
                            part[it, at, :] = total.astype(BF16)
                            send_a(at, way, k + 1, s, ring[way])
            def round_b(k):
                for way in (RIGHT, LEFT):
                    if k == 1:
                        @pl.when(b_long[way])
                        def _(way=way):
                            o = there(way, 4)
                            at = b_rows(yh, o)
                            part[it, at, :] = both_halves(at, o).astype(BF16)
                            send_b(at, way, 0, ring2[way])

                        o = there(way, 3)
                        at = b_rows(yh, o)
                        part[it, at, :] = both_halves(at, o).astype(BF16)
                        send_b(at, way, 1, ring[way])
                    elif k > 1:
                        o = there(way, 4 - k)
                        at = b_rows(yh, o)
                        total = both_halves(at, o) + add_b(way, k - 1)
                        part[it, at, :] = total.astype(BF16)
                        if k == 2:
                            @pl.when(b_long[way])
                            def _(way=way, at=at):
                                part[it, at, :] = (part[it, at, :].astype(F32) + add_b(way, 0)).astype(BF16)
                        send_b(at, way, k, ring[way])

            if k == 0:
                round_a(k)
            else:
                round_b(k)

            @pl.when(first)
            def _(k=k):
                f_step(2 * k)

            if k == 0:
                part[it, mine, :] = nt(t2[mine, :], fit[...]).astype(BF16)
                acc[...] = jnp.zeros_like(acc)
            if k > 0:
                round_a(k)

            @pl.when(first)
            def _(k=k):
                f_step(2 * k + 1)
                b_step(k)

        for s in range(2):
            at = a_rows(z, s)
            for way in (RIGHT, LEFT):
                arrived(rsa.at[it, way, 3, s], rsa_sem.at[it, way, 3, s])
            yv[it, s] = (
                part[it, at, :].astype(F32)
                + rsa[it, RIGHT, 3, s].astype(F32)
                + rsa[it, LEFT, 3, s].astype(F32)
            ).astype(BF16)
            send(yv.at[it, s], yr.at[it, s], y_send.at[it], y_sem.at[it, 1, s], y_far)

        @pl.when(first)
        def _():
            f_step(8)
            f_over(8)

        def own_sends(ref, sems):
            for way in (RIGHT, LEFT):
                send(ref, ref, ag_send.at[it], sems[way], ring[way])

        def to_far(ref, o):
            send(ref, ref, y_send.at[it], y_sem.at[it, 2, o], y_far)

        at = b_rows(yh, z)
        arrived(yfirst.at[it, z], y_sem.at[it, 0, z])
        for way in (RIGHT, LEFT):
            arrived(rsb.at[it, way, 3], rsb_sem.at[it, way, 3])
        pp[it, 0, at, :] = (
            part[it, at, :].astype(F32) + yfirst[it, z].astype(F32)
            + rsb[it, RIGHT, 3].astype(F32) + rsb[it, LEFT, 3].astype(F32)
        ).astype(BF16)
        own_sends(pp.at[it, 0, at], [agb_sem.at[it, way, 0] for way in (RIGHT, LEFT)])
        to_far(pp.at[it, 0, at], z)
        for s in range(2):
            at = a_rows(z, s)
            arrived(yr.at[it, s], y_sem.at[it, 1, s])
            pp[it, 0, at, :] = (yv[it, s].astype(F32) + yr[it, s].astype(F32)).astype(BF16)
            own_sends(pp.at[it, 0, at], [aga_sem.at[it, way, 0, s] for way in (RIGHT, LEFT)])

        def sent_on(ref, way, n, long, sems):
            @pl.when(n < 3)
            def _():
                send(ref, ref, ag_send.at[it], sems(n), ring[way])

            @pl.when(jnp.logical_and(n == 2, long))
            def _():
                send(ref, ref, ag_send.at[it], sems(3), ring2[way])

        def group(m, act):
            act(lax.rem(z + ZN - m, ZN))

            @pl.when(m >= 1)
            def _():
                act(lax.rem(z + m, ZN))

            @pl.when(m == 3)
            def _():
                act(lax.rem(z + 4, ZN))

        def relay(o):
            for at, index in (
                (a_rows(o, 1 - far_plane), (1 - far_plane) * 16 + o),
                (b_rows(1 - yl, o), (1 - far_plane) * 16 + 8 + o),
            ):
                ref, sem = pp.at[it, 1, at], bc_sem.at[it, index]
                arrived(ref, sem)
                send(ref, ref, bc_send.at[it, 5], sem, mate)

        @pl.loop(0, 6)
        def _(n):
            @pl.when(jnp.logical_and(n >= 1, n <= 3))
            def _():
                for way in (RIGHT, LEFT):
                    o = lax.rem(z + n * toward[1 - way], ZN)
                    ref = pp.at[it, 0, b_rows(yh, o)]
                    arrived(ref, agb_sem.at[it, way, n - 1])
                    sent_on(ref, way, n, b_long[way], lambda h, way=way: agb_sem.at[it, way, h])
                    to_far(ref, o)
                for s in range(2):
                    for way in (RIGHT, LEFT):
                        o = lax.rem(z + n * toward[1 - way], ZN)
                        ref = pp.at[it, 0, a_rows(o, s)]
                        arrived(ref, aga_sem.at[it, way, n - 1, s])
                        sent_on(ref, way, n, s == way, lambda h, way=way, s=s: aga_sem.at[it, way, h, s])

            @pl.when(n == 3)
            def _():
                o = lax.rem(z + 4, ZN)
                for way in (RIGHT, LEFT):
                    @pl.when(b_long[way])
                    def _(way=way):
                        ref = pp.at[it, 0, b_rows(yh, o)]
                        arrived(ref, agb_sem.at[it, way, 3])
                        to_far(ref, o)
                    arrived(pp.at[it, 0, a_rows(o, way)], aga_sem.at[it, way, 3, way])

            @pl.when(first)
            def _():
                f_step(9 + 2 * n)
                f_over(9 + 2 * n)

            @pl.when(jnp.logical_and(is_src, n <= 3))
            def _():
                def act(o):
                    for at, index in (
                        (a_rows(o, far_plane), far_plane * 16 + o),
                        (b_rows(yh, o), far_plane * 16 + 8 + o),
                    ):
                        src, dst, sem = pp.at[it, 0, at], pp.at[it, 1, at], bc_sem.at[it, index]
                        for shift in range(1, XN):
                            send(src, dst, bc_send.at[it, shift], sem, plane_peer(far_plane, shift))

                        @pl.when(far_plane == 1)
                        def _():
                            send(src, dst, bc_send.at[it, 0], sem, plane_peer(1, 0))

                group(n, act)

            m = n - 2 * sel

            @pl.when(jnp.logical_and(on_lane, jnp.logical_and(m >= 0, m <= 3)))
            def _():
                def act(o):
                    for at, index in (
                        (a_rows(o, far_plane), far_plane * 16 + o),
                        (b_rows(yl, o), far_plane * 16 + 8 + o),
                    ):
                        src, dst, sem = pp.at[it, sel, at], pp.at[it, 1, at], bc_sem.at[it, index]

                        @pl.when(sel == 1)
                        def _():
                            arrived(dst, sem)

                        send(src, dst, bc_send.at[it, 4], sem, y_near)
                        send(src, dst, bc_send.at[it, 6], sem, mate)

                group(m, act)

            @pl.when(jnp.logical_and(on_lane, n >= 4))
            def _():
                @pl.loop(n - 4, 2 * n - 7)
                def _(m):
                    group(m, relay)

            @pl.when(first)
            def _():
                f_step(10 + 2 * n)
                f_over(10 + 2 * n)
                b_step(n + 4)

            @pl.when(n >= 2)
            def _():
                start = lax.rem(core * 8 + (n - 2) * 4, 16)
                bb = bs[pl.ds(start, 4)].reshape(4 * virtual, virtual)
                for p in range(4):
                    i, j = p // 2, p % 2
                    con[p] = nn(
                        bb, t2[i * virtual:(i + 1) * virtual, j * virtual:(j + 1) * virtual]
                    ).astype(BF16)
                for p in range(4):
                    total = acc[p]
                    for k in range(4):
                        total = total + nt(con[p, k * virtual:(k + 1) * virtual, :], bb[k * virtual:(k + 1) * virtual])
                    acc[p] = total

            @pl.when(n == 5)
            def _():
                for o in range(ZN):
                    arrived(pp.at[it, 0, b_rows(1 - yh, o)], y_sem.at[it, 2, o])

            @pl.when(n >= 4)
            def _():
                i = n - 4
                term = nn(pp[it, 0, pl.ds(pl.multiple_of(i * virtual, virtual), virtual), :], fit[...])
                for j in range(2):
                    acc[2 * i + j] += term[:, j * virtual:(j + 1) * virtual]

        @pl.when(first)
        def _():
            @pl.loop(21, 26)
            def _(k):
                f_step(k)
                f_over(k)

            for way in (RIGHT, LEFT):
                for p in range(FP):
                    arrived(f_ref(fr, 1 - yh, way, p), f_sem.at[1, way, p])

        @pl.when(on_lane)
        def _():
            group(3, relay)

        for path in range(2):
            @pl.when(jnp.logical_not(on_lane))
            def _(path=path):
                for o in range(ZN):
                    arrived(pp.at[it, 1, a_rows(o, path)], bc_sem.at[it, path * 16 + o])
                    half = yh if path == 0 else 1 - yh
                    arrived(pp.at[it, 1, b_rows(half, o)], bc_sem.at[it, path * 16 + 8 + o])

        @pl.when(first)
        def _():
            exchange.wait()

        for i in range(2):
            term = tt(fr[:, i * virtual:(i + 1) * virtual], pp[it, sel])
            for j in range(2):
                total = coul[i, j].astype(F32) + acc[2 * i + j] + term[:, j * virtual:(j + 1) * virtual]
                denominator = (eps[row * 2 + i] + eps[col * 2 + j]) - ev_col[...] - ev_row[...]
                updated = (total / denominator).astype(BF16)
                t2[i * virtual:(i + 1) * virtual, j * virtual:(j + 1) * virtual] = updated
                out[i, j] = updated

        def left(pieces, sem):
            arrived(part.at[it, pl.ds(0, pieces * sub)], sem)

        left(21, rs_send.at[it])
        left(21, ag_send.at[it])
        left(18, y_send.at[it])

        @pl.when(on_lane)
        def _():
            for way in range(4, 7):
                left(16, bc_send.at[it, way])

        @pl.when(is_src)
        def _():
            for way in range(1, 4):
                left(16, bc_send.at[it, way])

            @pl.when(far_plane == 1)
            def _():
                left(16, bc_send.at[it, 0])

    def f_left(pieces, sem):
        arrived(fr.at[pl.ds(0, pieces * f_rows)], sem)

    for way, d in ((RIGHT, d_right), (LEFT, d_left)):
        @pl.when(d < ZN - 1)
        def _(way=way):
            f_left(FP, f_send.at[way])

    @pl.when(jnp.logical_and(is_seed, far_plane == 1))
    def _():
        f_left(2 * FP, f_send.at[2])

    f_left(2 * FP, f_send.at[3])
    arrived(block(x, yl), b_send.at[0])
    arrived(pair(x), b_send.at[1])
    arrived(pair(x), b_send.at[2])
    arrived(block(x, yl), b_send.at[3])
    arrived(block(x, yl), b_send.at[4])
    arrived(bs.at[pl.ds(core * 8, 8)], b_send.at[5])


def body(amplitudes, coulomb, fit_ov, fit_vv, eps_occ, eps_vir):
    occ_local, occ_other, virtual, _ = amplitudes.shape
    aux = fit_ov.shape[0]
    side = occ_local * virtual
    sub = side // (4 * ZN)
    fit = fit_ov.reshape(aux, occ_other * virtual)
    batch = fit_vv.shape[0] * lax.axis_size("row")
    vmem = pl.BlockSpec(memory_space=pltpu.VMEM)
    dma = pltpu.SemaphoreType.DMA
    return pl.pallas_call(
        kernel,
        out_shape=jax.ShapeDtypeStruct(amplitudes.shape, BF16),
        in_specs=[pl.BlockSpec(memory_space=pltpu.SMEM)] + [vmem, pl.BlockSpec(memory_space=pl.ANY)] + [vmem] * 3,
        out_specs=vmem,
        scratch_shapes=[
            pltpu.VMEM((side, occ_other * virtual), BF16),
            pltpu.VMEM((ITERS, side, aux), BF16),
            pltpu.VMEM((ITERS, 2, 4, 2, sub, aux), BF16),
            pltpu.VMEM((ITERS, 2, 4, sub, aux), BF16),
            pltpu.VMEM((ITERS, ZN, sub, aux), BF16),
            pltpu.VMEM((ITERS, 2, sub, aux), BF16),
            pltpu.VMEM((ITERS, 2, sub, aux), BF16),
            pltpu.VMEM((ITERS, 2, side, aux), BF16),
            pltpu.VMEM((aux, side), BF16),
            pltpu.VMEM((batch, virtual, virtual), BF16),
            pltpu.VMEM((occ_local * occ_other, virtual, virtual), F32),
            pltpu.VMEM((4, 4 * virtual, virtual), BF16),
            pltpu.VMEM((virtual, virtual), F32),
            dma((ITERS, 2, 4, 2)),
            dma((ITERS, 2, 4)),
            dma((ITERS, 3, ZN)),
            dma((ITERS, 2, 4, 2)),
            dma((ITERS, 2, 4)),
            dma((ITERS, 4 * ZN)),
            dma((2, 2, FP)),
            dma((6,)),
            dma((ITERS,)),
            dma((ITERS,)),
            dma((ITERS,)),
            dma((ITERS, 7)),
            dma((4,)),
            dma((6,)),
            dma,
            pltpu.VMEM(coulomb.shape, BF16),
            dma,
        ],
        compiler_params=pltpu.CompilerParams(
            collective_id=0, has_side_effects=True, vmem_limit_bytes=60 * 2**20
        ),
        name="sweeps",
    )(eps_occ, amplitudes, coulomb, fit, fit_vv, eps_vir[None, :])


def solution(mesh):
    in_specs = (
        P("row", "col", None, None),
        P("row", "col", None, None),
        P(None, "col", None),
        P("row", None, None),
        P(),
        P(),
    )
    out_specs = P("row", "col", None, None)
    return jax.shard_map(body, mesh=mesh, in_specs=in_specs, out_specs=out_specs, check_vma=False)
```
